32 devices in a mesh: groups: 2 (over x), seq: 16 (over z, y, core).
Axes of the slice: x: 2, y: 2, z: 4, core: 2. Of those that a mesh axis runs over, the one named last changes fastest.
Arguments:
- queries: bfloat16 [8192, 2048], P(('groups', 'seq')), parts along dimension 0, may hold values from -400 to 400
- neighbours: bfloat16 [64, 128, 896], P(('groups', 'seq')), parts along dimension 0, may hold values from -500 to 500
- w_key: bfloat16 [896, 2048], replicated, may hold values from -0.1875 to 0.1875
- w_value: bfloat16 [896, 2048], replicated, may hold values from -0.1875 to 0.1875
- retrieval_owner: int32 [128, 2], P(('groups', 'seq')), parts along dimension 0, may hold values from 0 to 15, as said below
- retrieval_slot: int32 [128, 2], P(('groups', 'seq')), parts along dimension 0, may hold values from 0 to 1
- doc_starts: int32 [128], P(('groups', 'seq')), parts along dimension 0, may hold values 0 or 1
Outputs:
- attended: bfloat16 [8192, 2048], P(('groups', 'seq')), parts along dimension 0
The draws below stay inside these ranges and needn't reach their ends.
There are 2 independent parts, one for each index of `groups`. The reference program is written for one: setup_inputs(seed, part) draws one part's arguments, and reference() takes and returns one part's arrays. A program takes and returns all parts, laid end to end along the dimension named above; an argument that names none is the same for every part. Nothing has to cross between parts.
Inputs may be any that keep to these rules, and one draw needn't show every extreme that they name: `retrieval_owner`: among the 8 owners named by the spans of one device, no owner appears more than 1 times, and some owner appears exactly 1 times.
All inputs are finite; a program needn't handle non-finite values. No bound on the sum of `doc_starts` on one device may be relied on, other than what follows from the above.
Results may differ from the reference program's by a relative error of at most 0.0071.
Values may be sent and summed in bfloat16 or wider, within the bound.
A program may use at most 128 MiB of HBM per device.

```python
import math
import jax
import jax.numpy as jnp
from jax import lax

CH_DEV = 4
SPAN = 64
NBLEN = 128
NW = 896
HEADS = 16
HEAD_DIM = 128
CAP = 1
NB_DEV = 2
TOKENS = 4096
SPANS = 64
N_SEQ = 16


def draw_queries(key, part):
    shape = (TOKENS, HEADS * HEAD_DIM)
    return jax.random.truncated_normal(key, -4.0, 4.0, shape, jnp.float32).astype(jnp.bfloat16)


def draw_neighbours(key, part):
    shape = (NB_DEV * N_SEQ, NBLEN, NW)
    core_key, row_key, col_key = jax.random.split(key, 3)
    row_scale = jnp.exp(jax.random.uniform(row_key, (NB_DEV * N_SEQ, NBLEN, 1), jnp.float32, 0.0, math.log(10.0)))
    col_scale = jnp.exp(jax.random.uniform(col_key, (1, 1, NW), jnp.float32, 0.0, math.log(10.0)))
    core = jax.random.truncated_normal(core_key, -4.0, 4.0, shape, jnp.float32)
    return (core * row_scale * col_scale).astype(jnp.bfloat16)


def owner_list(key, device, hot_owner):
    device_key = jax.random.fold_in(key, device)
    shuffled = jax.random.permutation(device_key, N_SEQ)
    leading = shuffled[0]
    shuffled = jnp.where(shuffled == hot_owner, leading, shuffled)
    shuffled = jnp.where(jnp.arange(N_SEQ) == 0, hot_owner, shuffled)
    repeated = jnp.tile(shuffled, CAP)[:2 * CH_DEV]
    order = jax.random.permutation(jax.random.fold_in(device_key, 7), 2 * CH_DEV)
    return repeated[order]


def draw_retrieval_owner(key, part):
    hot_owner = jax.random.randint(jax.random.fold_in(key, 3), (), 0, N_SEQ)
    lists = jax.vmap(lambda device: owner_list(key, device, hot_owner))(jnp.arange(N_SEQ))
    return lists.reshape(CH_DEV * N_SEQ, 2).astype(jnp.int32)


def touch_ends(entries, own_key, least, top_value):
    index_at = [jax.random.randint(jax.random.fold_in(own_key, axis), (), 0, length) for axis, length in enumerate(entries.shape)]
    widest = entries.shape.index(max(entries.shape))
    beside = index_at[:widest] + [(index_at[widest] + 1) % entries.shape[widest]] + index_at[widest + 1:]
    return entries.at[tuple(index_at)].set(least).at[tuple(beside)].set(top_value)


def scatter_about(rng, dims, scale, limit, held_as=jnp.bfloat16):
    values = scale * jax.random.normal(rng, dims, jnp.float32)
    return jnp.clip(values, min=-limit, max=limit).astype(held_as)


def setup_inputs(seed: int = 0, part: int = 0) -> dict:
    streams_of = jax.random.split(jax.random.key(seed), 8)
    part_splits = jax.random.split(jax.random.fold_in(streams_of[7], part), 8)
    queries = draw_queries(jax.random.fold_in(jax.random.fold_in(streams_of[7], part), 71), part)
    neighbours = draw_neighbours(jax.random.fold_in(jax.random.fold_in(streams_of[7], part), 71), part)
    w_key = scatter_about(streams_of[2], (NW, HEADS * HEAD_DIM), NW ** -0.5, 0.1875)
    w_value = scatter_about(streams_of[3], (NW, HEADS * HEAD_DIM), NW ** -0.5, 0.1875)
    retrieval_owner = draw_retrieval_owner(jax.random.fold_in(jax.random.fold_in(streams_of[7], part), 71), part)
    retrieval_slot = touch_ends(jax.random.randint(part_splits[5], (SPANS, 2), 0, NB_DEV), jax.random.fold_in(part_splits[5], 1), 0, NB_DEV - 1).astype(jnp.int32)
    doc_starts = touch_ends((jax.random.randint(part_splits[6], (SPANS,), 0, 4) < 1).astype(jnp.int32), jax.random.fold_in(part_splits[6], 1), 0, 1)
    return {"queries": queries, "neighbours": neighbours, "w_key": w_key, "w_value": w_value, "retrieval_owner": retrieval_owner, "retrieval_slot": retrieval_slot, "doc_starts": doc_starts}


def normalize(tokens_in):
    widened = tokens_in.astype(jnp.float32)
    factor = lax.rsqrt(lax.optimization_barrier(jnp.mean(widened * widened, axis=-1, keepdims=True)) + 1e-06)
    return (widened * factor).astype(jnp.bfloat16)

def reference(queries, neighbours, w_key, w_value, retrieval_owner, retrieval_slot, doc_starts):
    model_width = HEADS * HEAD_DIM
    token_count = queries.shape[0]
    span_count = doc_starts.shape[0]
    normed = normalize(neighbours).reshape(-1, NW)
    keys_all = jnp.dot(normed, w_key, preferred_element_type=jnp.float32).astype(jnp.bfloat16).reshape(-1, NBLEN, model_width)
    values_all = jnp.dot(normed, w_value, preferred_element_type=jnp.float32).astype(jnp.bfloat16).reshape(-1, NBLEN, model_width)
    neighbour_ids = (retrieval_owner * NB_DEV + retrieval_slot).astype(jnp.int32)
    shifted = jnp.concatenate([queries[SPAN - 1:], jnp.zeros((SPAN - 1, model_width), jnp.bfloat16)], 0)
    shifted = shifted.reshape(span_count, SPAN, model_width)
    later = jnp.concatenate([doc_starts[1:], jnp.ones((1,), jnp.int32)])
    row_index = jnp.arange(SPAN)
    valid = (row_index[None, :] == 0) | (later[:, None] == 0)
    score_scale = 1.0 / jnp.sqrt(jnp.float32(HEAD_DIM))

    def window(packed):
        query_block, pair_ids, kept = packed
        key_block = keys_all[pair_ids].reshape(2 * NBLEN, HEADS, HEAD_DIM).astype(jnp.float32)
        value_block = values_all[pair_ids].reshape(2 * NBLEN, HEADS, HEAD_DIM).astype(jnp.float32)
        query_heads = query_block.reshape(SPAN, HEADS, HEAD_DIM).astype(jnp.float32)
        scores = jnp.einsum('qhd,khd->hqk', query_heads, key_block) * score_scale
        highest = lax.optimization_barrier(jnp.max(scores, axis=-1, keepdims=True))
        powers = jnp.exp(scores - highest)
        totals = lax.optimization_barrier(jnp.sum(powers, axis=-1, keepdims=True))
        weights = lax.optimization_barrier((powers / totals).astype(jnp.bfloat16)).astype(jnp.float32)
        result = jnp.einsum('hqk,khd->qhd', weights, value_block).reshape(SPAN, model_width)
        result = jnp.where(kept[:, None], result, 0.0)
        return result.astype(jnp.bfloat16)
    outputs = lax.map(window, (shifted, neighbour_ids, valid))
    flattened = outputs.reshape(token_count, model_width)
    return jnp.concatenate([jnp.zeros((SPAN - 1, model_width), jnp.bfloat16), flattened[:token_count - SPAN + 1]], 0)
```

```python
import math

import jax
import jax.numpy as jnp
from jax import lax
from jax.sharding import PartitionSpec as P

SPAN = 64
HEADS = 16
HEAD_DIM = 128


def from_behind(value, axis, steps):
    count = lax.axis_size(axis)
    first, last = (max(0, -steps), min(count, count - steps))
    return lax.ppermute(value, axis, [(source, source + steps) for source in range(first, last)])


def normalize(tokens_in):
    widened = tokens_in.astype(jnp.float32)
    factor = lax.rsqrt(jnp.mean(widened * widened, axis=-1, keepdims=True) + 1e-06)
    return (widened * factor).astype(jnp.bfloat16)


def project(chosen, w_key, w_value, span_count):
    model_width = w_key.shape[1]
    normed = normalize(chosen).reshape(-1, chosen.shape[-1])
    key_rows = jnp.dot(normed, w_key, preferred_element_type=jnp.float32).astype(jnp.bfloat16)
    value_rows = jnp.dot(normed, w_value, preferred_element_type=jnp.float32).astype(jnp.bfloat16)
    return (
        key_rows.reshape(span_count, -1, model_width),
        value_rows.reshape(span_count, -1, model_width),
    )


def attend(query_rows, key_rows, value_rows):
    windows = query_rows.shape[0]
    query_heads = query_rows.reshape(windows, SPAN, HEADS, HEAD_DIM)
    key_heads = key_rows.reshape(windows, -1, HEADS, HEAD_DIM)
    value_heads = value_rows.reshape(windows, -1, HEADS, HEAD_DIM)
    scores = jnp.einsum(
        "wqhd,wkhd->whqk", query_heads, key_heads, preferred_element_type=jnp.float32
    )
    scores = scores * (1.0 / math.sqrt(HEAD_DIM))
    highest = jnp.max(scores, axis=-1, keepdims=True)
    powers = jnp.exp(scores - highest)
    totals = jnp.sum(powers, axis=-1, keepdims=True)
    weights = (powers / totals).astype(jnp.bfloat16)
    result = jnp.einsum("whqk,wkhd->wqhd", weights, value_heads, preferred_element_type=jnp.float32)
    return result.reshape(windows * SPAN, HEADS * HEAD_DIM).astype(jnp.bfloat16)


def body(queries, neighbours, w_key, w_value, retrieval_owner, retrieval_slot, doc_starts):
    span_count = doc_starts.shape[0]
    token_count = queries.shape[0]
    model_width = queries.shape[1]
    stored = lax.all_gather(neighbours, "seq", axis=0, tiled=True)
    wanted = (retrieval_owner * neighbours.shape[0] + retrieval_slot).reshape(-1)
    chosen = jnp.take(stored, wanted, axis=0)
    key_rows, value_rows = project(chosen, w_key, w_value, span_count)
    tail_rows = from_behind(queries[: SPAN - 1], "seq", -1)
    query_rows = jnp.concatenate([queries[SPAN - 1 :], tail_rows], 0).reshape(
        span_count, SPAN, model_width
    )
    computed = attend(query_rows, key_rows, value_rows)
    head_rows = from_behind(computed[token_count - SPAN + 1 :], "seq", 1)
    attended = jnp.concatenate([head_rows, computed[: token_count - SPAN + 1]], 0)
    offsets = jnp.arange(SPAN)
    fresh_rows = (doc_starts[:, None] == 0) | (offsets[None, :] == SPAN - 1)
    opening = (
        (lax.axis_index("seq") == 0)
        & (jnp.arange(span_count)[:, None] == 0)
        & (offsets[None, :] < SPAN - 1)
    )
    kept_rows = (fresh_rows & jnp.logical_not(opening)).reshape(token_count)
    return jnp.where(kept_rows[:, None], attended, jnp.zeros((), jnp.bfloat16))


def solution(mesh):
    return jax.shard_map(
        body,
        mesh=mesh,
        in_specs=(
            P(("groups", "seq"), None),
            P(("groups", "seq"), None, None),
            P(),
            P(),
            P(("groups", "seq"), None),
            P(("groups", "seq"), None),
            P(("groups", "seq")),
        ),
        out_specs=P(("groups", "seq"), None),
        check_vma=False,
    )
```

```python
import functools
import math

import jax
import jax.numpy as jnp
from jax import lax
from jax.experimental import pallas as pl
from jax.experimental.pallas import tpu as pltpu
from jax.sharding import PartitionSpec as P

SPAN = 64
HEADS = 16
HEAD_DIM = 128
CHUNKS = 4
TAIL = 16
COLS = 256
UNROLL = 4


def ring_depth(mesh):
    devices = mesh.devices.reshape(mesh.shape["groups"], mesh.shape["seq"])[0]
    spots = [getattr(d, "coords", None) for d in devices[::2]]
    if any(s is None for s in spots) or len(spots) < 4:
        return 1
    spots = [tuple(s) for s in spots]
    apart = lambda a, b: {k for k in range(3) if a[k] != b[k]}
    return 2 if apart(spots[0], spots[1]).isdisjoint(apart(spots[0], spots[2])) else 1


def place_of(chip, chips, depth):
    if depth == 1:
        return chip
    far = chips // 2
    z, y = chip // 2, chip % 2
    return jnp.where(y == 0, z, 2 * far - 1 - z)


def chip_at(place, chips, depth):
    if depth == 1:
        return place
    far = chips // 2
    return jnp.where(place < far, 2 * place, 2 * (2 * far - 1 - place) + 1)


def kernel(
    n, depth,
    ids_s, ids_v, q_ref, nb_ref, wk_ref, wv_ref, out_ref,
    *scratch,
):
    gats = scratch[:CHUNKS]
    (w_ref, kv_ref, xn_ref, prev_v, prev_s,
     ring_recv, ring_send, pair_recv, pair_send, own_sem, w_sem, id_sem) = scratch[CHUNKS:]
    slots, length, width = nb_ref.shape
    rows = length // CHUNKS
    windows = kv_ref.shape[0]
    model = wk_ref.shape[1]
    requests = 2 * (windows - 1)
    chips = n // 2
    half = chips // 2

    me = lax.axis_index("seq")
    core = me % 2
    partner = me + 1 - 2 * core
    place = place_of(me // 2, chips, depth)

    def device_at(p):
        return chip_at((p + chips) % chips, chips, depth) * 2 + core

    right, left = device_at(place + 1), device_at(place - 1)
    nxt, prv = (me + 1) % n, (me + n - 1) % n

    w_copies = [
        pltpu.make_async_copy(wk_ref, w_ref.at[:, pl.ds(0, model)], w_sem.at[0]),
        pltpu.make_async_copy(wv_ref, w_ref.at[:, pl.ds(model, model)], w_sem.at[1]),
    ]
    own_copies = [
        pltpu.make_async_copy(
            nb_ref.at[:, pl.ds(g * rows, rows), :], gats[g].at[pl.ds(slots * me, slots)], own_sem.at[g]
        )
        for g in range(CHUNKS)
    ]

    barrier = pltpu.get_barrier_semaphore()
    for other in (left, right, partner, nxt, prv):
        pl.semaphore_signal(barrier, inc=1, device_id={"seq": other}, device_id_type=pl.DeviceIdType.MESH)
    pl.semaphore_wait(barrier, 5)

    id_copy = pltpu.make_async_remote_copy(
        src_ref=ids_v, dst_ref=prev_v, send_sem=id_sem.at[0], recv_sem=id_sem.at[1],
        device_id={"seq": nxt}, device_id_type=pl.DeviceIdType.MESH,
    )

    def ring_copy(g, d, way, slot):
        origin = device_at(place - (d - 1) if way == 0 else place + (d - 1))
        block = origin * slots + slot
        src = nb_ref.at[slot, pl.ds(g * rows, rows), :] if d == 1 else gats[g].at[block]
        return pltpu.make_async_remote_copy(
            src_ref=src, dst_ref=gats[g].at[block],
            send_sem=ring_send.at[g], recv_sem=ring_recv.at[g, d - 1, way, slot],
            device_id={"seq": right if way == 0 else left}, device_id_type=pl.DeviceIdType.MESH,
        )

    def pair_copy(g, d, way, slot):
        origin = device_at(place - d if way == 0 else place + d)
        block = origin * slots + slot
        src = nb_ref.at[slot, pl.ds(g * rows, rows), :] if d == 0 else gats[g].at[block]
        return pltpu.make_async_remote_copy(
            src_ref=src, dst_ref=gats[g].at[block],
            send_sem=pair_send.at[g], recv_sem=pair_recv.at[g],
            device_id={"seq": partner}, device_id_type=pl.DeviceIdType.MESH,
        )

    def items(d):
        return [(way, slot) for slot in range(slots) for way in range(2) if d < half or slot % 2 == way]

    def event(g, d):
        if d == 0:
            for way, slot in items(1):
                ring_copy(g, 1, way, slot).start()
            for slot in range(slots):
                pair_copy(g, 0, 0, slot).start()
            own_copies[g].start()
            return
        for way, slot in items(d):
            ring_copy(g, d, way, slot).wait_recv()
            if d < half and (way, slot) in items(d + 1):
                ring_copy(g, d + 1, way, slot).start()
            pair_copy(g, d, way, slot).start()

    def total(g, blocks, sem):
        part = gats[g].at[pl.ds(0, blocks)]
        return pltpu.make_async_copy(part, part, sem)

    def norm_piece(g):
        own_copies[g].wait()
        total(g, n * slots // 2, pair_recv.at[g]).wait()

        @pl.loop(0, requests + 2)
        def _(i):
            before = prev_s[0, requests - 2 + jnp.minimum(i, 1)]
            mine = ids_s[jnp.maximum(i - 2, 0)]
            x = gats[g][jnp.where(i < 2, before, mine)].astype(jnp.float32)
            factor = lax.rsqrt(jnp.mean(x * x, axis=-1, keepdims=True) + 1e-06)
            xn_ref[i] = (x * factor).astype(jnp.bfloat16)

    def proj_piece(g, part):
        xs = xn_ref.reshape(windows * 2 * rows, width)

        @pl.loop(0, model // COLS)
        def _(c):
            cols = pl.ds(pl.multiple_of(part * model + c * COLS, COLS), COLS)
            y = jnp.dot(xs[...], w_ref[:, cols], preferred_element_type=jnp.float32).astype(jnp.bfloat16)
            kv_ref[:, g * 2 * rows : (g + 1) * 2 * rows, cols] = y.reshape(windows, 2 * rows, COLS)

    stagger = max(half // 2, 1)
    order = sorted(
        ((stagger * g + d, g, d) for g in range(CHUNKS) for d in range(half + 1)),
    )
    id_copy.start()
    pending = []
    started = False
    for _, g, d in order:
        event(g, d)
        if not started:
            started = True
            for c in w_copies:
                c.start()
        if pending:
            pending.pop(0)()
        if g == 0 and d == half:
            id_copy.wait_recv()
            move = pltpu.make_async_copy(prev_v, prev_s, id_sem.at[2])
            move.start()
            move.wait()
            for c in w_copies:
                c.wait()
        if d == half:
            pending += [
                functools.partial(norm_piece, g),
                functools.partial(proj_piece, g, 0),
                functools.partial(proj_piece, g, 1),
            ]
    for piece in pending:
        piece()

    scale = 1.0 / math.sqrt(HEAD_DIM)

    def attend(w, start, count, h):
        cols = pl.ds(pl.multiple_of(h * HEAD_DIM, HEAD_DIM), HEAD_DIM)
        vcols = pl.ds(pl.multiple_of(model + h * HEAD_DIM, HEAD_DIM), HEAD_DIM)
        q = q_ref[pl.ds(start, count), cols]
        k = kv_ref[w, :, cols]
        v = kv_ref[w, :, vcols]
        s = lax.dot_general(q, k, (((1,), (1,)), ((), ())), preferred_element_type=jnp.float32) * scale
        p = jnp.exp(s - jnp.max(s, axis=-1, keepdims=True))
        p = (p / jnp.sum(p, axis=-1, keepdims=True)).astype(jnp.bfloat16)
        o = jnp.dot(p, v, preferred_element_type=jnp.float32)
        out_ref[pl.ds(start, count), cols] = o.astype(jnp.bfloat16)

    heads = model // HEAD_DIM

    @pl.loop(0, (windows - 1) * (heads // UNROLL))
    def _(t):
        w = t // (heads // UNROLL)
        for u in range(UNROLL):
            attend(w, pl.multiple_of(w * SPAN, SPAN), SPAN, (t % (heads // UNROLL)) * UNROLL + u)

    @pl.loop(0, heads // UNROLL)
    def _(t):
        for u in range(UNROLL):
            attend(windows - 1, (windows - 1) * SPAN, TAIL, t * UNROLL + u)

    id_copy.wait_send()
    for g in range(CHUNKS):
        total(g, (n - 2) * slots // 2, ring_send.at[g]).wait()
        total(g, n * slots // 2, pair_send.at[g]).wait()


def body(n, depth, queries, neighbours, w_key, w_value, retrieval_owner, retrieval_slot, doc_starts):
    span_count = doc_starts.shape[0]
    token_count, model = queries.shape
    slots, length, width = neighbours.shape
    windows = span_count + 1
    rows = length // CHUNKS
    chips = n // 2
    ids = (retrieval_owner * slots + retrieval_slot).reshape(-1)
    ids_wide = jnp.zeros((8, 128), jnp.int32).at[:, : 2 * span_count].set(ids[None, :])
    padded = jnp.pad(queries, ((1, TAIL - 1), (0, 0)))
    any_spec = pl.BlockSpec(memory_space=pl.ANY)
    vmem = pl.BlockSpec(memory_space=pltpu.VMEM)
    smem = pl.BlockSpec(memory_space=pltpu.SMEM)
    result = pl.pallas_call(
        functools.partial(kernel, n, depth),
        out_shape=jax.ShapeDtypeStruct((token_count + TAIL, model), jnp.bfloat16),
        in_specs=[smem, vmem, vmem, any_spec, any_spec, any_spec],
        out_specs=vmem,
        scratch_shapes=[pltpu.VMEM((n * slots, rows, width), jnp.bfloat16) for _ in range(CHUNKS)]
        + [
            pltpu.VMEM((width, 2 * model), jnp.bfloat16),
            pltpu.VMEM((windows, 2 * length, 2 * model), jnp.bfloat16),
            pltpu.VMEM((2 * windows, rows, width), jnp.bfloat16),
            pltpu.VMEM((8, 128), jnp.int32),
            pltpu.SMEM((8, 128), jnp.int32),
            pltpu.SemaphoreType.DMA((CHUNKS, chips // 2, 2, slots)),
            pltpu.SemaphoreType.DMA((CHUNKS,)),
            pltpu.SemaphoreType.DMA((CHUNKS,)),
            pltpu.SemaphoreType.DMA((CHUNKS,)),
            pltpu.SemaphoreType.DMA((CHUNKS,)),
            pltpu.SemaphoreType.DMA((2,)),
            pltpu.SemaphoreType.DMA((3,)),
        ],
        compiler_params=pltpu.CompilerParams(
            collective_id=0, has_side_effects=True, vmem_limit_bytes=60 * 1024 * 1024
        ),
    )(ids, ids_wide, padded, neighbours, w_key, w_value)
    attended = result[1 : token_count + 1]
    offsets = jnp.arange(SPAN)
    fresh_rows = (doc_starts[:, None] == 0) | (offsets[None, :] == SPAN - 1)
    opening = (
        (lax.axis_index("seq") == 0)
        & (jnp.arange(span_count)[:, None] == 0)
        & (offsets[None, :] < SPAN - 1)
    )
    kept_rows = (fresh_rows & jnp.logical_not(opening)).reshape(token_count)
    return jnp.where(kept_rows[:, None], attended, jnp.zeros((), jnp.bfloat16))


def solution(mesh):
    return jax.shard_map(
        functools.partial(body, mesh.shape["seq"], ring_depth(mesh)),
        mesh=mesh,
        in_specs=(
            P(("groups", "seq"), None),
            P(("groups", "seq"), None, None),
            P(),
            P(),
            P(("groups", "seq"), None),
            P(("groups", "seq"), None),
            P(("groups", "seq")),
        ),
        out_specs=P(("groups", "seq"), None),
        check_vma=False,
    )
```

```python
import functools
import math

import jax
import jax.numpy as jnp
from jax import lax
from jax.experimental import pallas as pl
from jax.experimental.pallas import tpu as pltpu
from jax.sharding import PartitionSpec as P

SPAN = 64
HEADS = 16
HEAD_DIM = 128
CHUNKS = 4
TAIL = 16
COLS = 256
UNROLL = 2
STAGGER = 1


def ring_depth(mesh):
    devices = mesh.devices.reshape(mesh.shape["groups"], mesh.shape["seq"])[0]
    spots = [getattr(d, "coords", None) for d in devices[::2]]
    if any(s is None for s in spots) or len(spots) < 4:
        return 1
    spots = [tuple(s) for s in spots]
    apart = lambda a, b: {k for k in range(3) if a[k] != b[k]}
    return 2 if apart(spots[0], spots[1]).isdisjoint(apart(spots[0], spots[2])) else 1


def place_of(chip, chips, depth):
    if depth == 1:
        return chip
    far = chips // 2
    z, y = chip // 2, chip % 2
    return jnp.where(y == 0, z, 2 * far - 1 - z)


def chip_at(place, chips, depth):
    if depth == 1:
        return place
    far = chips // 2
    return jnp.where(place < far, 2 * place, 2 * (2 * far - 1 - place) + 1)


def kernel(
    n, depth,
    owner_s, slot_s, doc_s, owner_v, slot_v, q_hbm, nb_ref, wk_ref, wv_ref, out_ref,
    *scratch,
):
    gats = scratch[:CHUNKS]
    (w_ref, kv_ref, xn_ref, q_raw, q_ref, keep_ref, prev_ov, prev_sv, prev_os, prev_ss,
     ring_recv, ring_send, pair_recv, pair_send, own_sem, w_sem, id_sem, q_sem) = scratch[CHUNKS:]
    slots, length, width = nb_ref.shape
    rows = length // CHUNKS
    windows = kv_ref.shape[0]
    spans = windows - 1
    model = wk_ref.shape[1]
    chips = n // 2
    half = chips // 2

    me = lax.axis_index("seq")
    core = me % 2
    partner = me + 1 - 2 * core
    place = place_of(me // 2, chips, depth)

    def device_at(p):
        return chip_at((p + chips) % chips, chips, depth) * 2 + core

    right, left = device_at(place + 1), device_at(place - 1)
    nxt, prv = (me + 1) % n, (me + n - 1) % n

    w_copies = [
        pltpu.make_async_copy(wk_ref, w_ref.at[:, pl.ds(0, model)], w_sem.at[0]),
        pltpu.make_async_copy(wv_ref, w_ref.at[:, pl.ds(model, model)], w_sem.at[1]),
    ]
    own_copies = [
        pltpu.make_async_copy(
            nb_ref.at[:, pl.ds(g * rows, rows), :], gats[g].at[pl.ds(slots * me, slots)], own_sem.at[g]
        )
        for g in range(CHUNKS)
    ]

    q_copy = pltpu.make_async_copy(q_hbm, q_raw, q_sem)

    barrier = pltpu.get_barrier_semaphore()
    for other in (left, right, partner, nxt, prv):
        pl.semaphore_signal(barrier, inc=1, device_id={"seq": other}, device_id_type=pl.DeviceIdType.MESH)
    pl.semaphore_wait(barrier, 5)

    id_copies = [
        pltpu.make_async_remote_copy(
            src_ref=src, dst_ref=dst, send_sem=id_sem.at[k, 0], recv_sem=id_sem.at[k, 1],
            device_id={"seq": nxt}, device_id_type=pl.DeviceIdType.MESH,
        )
        for k, (src, dst) in enumerate(((owner_v, prev_ov), (slot_v, prev_sv)))
    ]
    id_moves = [
        pltpu.make_async_copy(prev_ov, prev_os, id_sem.at[0, 2]),
        pltpu.make_async_copy(prev_sv, prev_ss, id_sem.at[1, 2]),
    ]

    def share(g, origin, slot, count, own):
        block = origin * slots + slot
        if own:
            return nb_ref.at[pl.ds(slot, count), pl.ds(g * rows, rows), :], gats[g].at[pl.ds(block, count)]
        return gats[g].at[pl.ds(block, count)], gats[g].at[pl.ds(block, count)]

    def ring_copy(g, d, way):
        origin = device_at(place - (d - 1) if way == 0 else place + (d - 1))
        slot, count = (0, slots) if d < half else (way * slots // 2, slots // 2)
        src, dst = share(g, origin, slot, count, d == 1)
        return pltpu.make_async_remote_copy(
            src_ref=src, dst_ref=dst,
            send_sem=ring_send.at[g], recv_sem=ring_recv.at[g, d - 1, way],
            device_id={"seq": right if way == 0 else left}, device_id_type=pl.DeviceIdType.MESH,
        )

    def pair_copy(g, d, way):
        origin = device_at(place - d if way == 0 else place + d)
        slot, count = (0, slots) if d < half else (way * slots // 2, slots // 2)
        src, dst = share(g, origin, slot, count, d == 0)
        return pltpu.make_async_remote_copy(
            src_ref=src, dst_ref=dst,
            send_sem=pair_send.at[g], recv_sem=pair_recv.at[g],
            device_id={"seq": partner}, device_id_type=pl.DeviceIdType.MESH,
        )

    def event(g, d):
        if d == 0:
            for way in range(2):
                ring_copy(g, 1, way).start()
            pair_copy(g, 0, 0).start()
            own_copies[g].start()
            return
        for way in range(2):
            ring_copy(g, d, way).wait_recv()
            if d < half:
                ring_copy(g, d + 1, way).start()
            pair_copy(g, d, way).start()

    def total(g, blocks, sem):
        part = gats[g].at[pl.ds(0, blocks)]
        return pltpu.make_async_copy(part, part, sem)

    def norm_piece(g):
        own_copies[g].wait()
        total(g, n * slots // 2, pair_recv.at[g]).wait()

        @pl.loop(0, 2 * windows)
        def _(i):
            span, j = jnp.maximum(i // 2 - 1, 0), i % 2
            before = prev_os[spans - 1, j] * slots + prev_ss[spans - 1, j]
            mine = owner_s[span, j] * slots + slot_s[span, j]
            x = gats[g][jnp.where(i < 2, before, mine)].astype(jnp.float32)
            factor = lax.rsqrt(jnp.mean(x * x, axis=-1, keepdims=True) + 1e-06)
            xn_ref[i] = (x * factor).astype(jnp.bfloat16)

    def proj_piece(g, part):
        xs = xn_ref.reshape(windows * 2 * rows, width)

        @pl.loop(0, model // COLS)
        def _(c):
            cols = pl.ds(pl.multiple_of(part * model + c * COLS, COLS), COLS)
            y = jnp.dot(xs[...], w_ref[:, cols], preferred_element_type=jnp.float32).astype(jnp.bfloat16)
            kv_ref[:, g * 2 * rows : (g + 1) * 2 * rows, cols] = y.reshape(windows, 2 * rows, COLS)

    def shift_piece():
        q_copy.wait()

        @pl.loop(0, model // COLS)
        def _(c):
            cols = pl.ds(pl.multiple_of(c * COLS, COLS), COLS)
            q_ref[:, cols] = pltpu.roll(q_raw[:, cols].astype(jnp.float32), 1, 0).astype(jnp.bfloat16)

        at = lax.broadcasted_iota(jnp.int32, (SPAN, HEAD_DIM), 0)
        for c in range(spans):
            open_row = (1 - doc_s[c]).astype(jnp.float32)
            if c == 0:
                open_row = jnp.where(me == 0, 0.0, open_row)
            keep_ref[c * SPAN : (c + 1) * SPAN, :] = jnp.where(at == SPAN - 1, 1.0, open_row)

    def id_piece():
        for copy, move in zip(id_copies, id_moves):
            copy.wait_recv()
            move.start()
        for move in id_moves:
            move.wait()
        for c in w_copies:
            c.wait()

    order = sorted(
        ((STAGGER * g + d, g, d) for g in range(CHUNKS) for d in range(half + 1)),
    )
    for copy in id_copies:
        copy.start()
    pending = []
    for at, (_, g, d) in enumerate(order):
        event(g, d)
        if at == 0:
            q_copy.start()
            for c in w_copies:
                c.start()
            pending = [shift_piece, id_piece]
        elif pending:
            pending.pop(0)()
        if d == half:
            pending += [
                functools.partial(norm_piece, g),
                functools.partial(proj_piece, g, 0),
                functools.partial(proj_piece, g, 1),
            ]
    for piece in pending:
        piece()

    scale = math.log2(math.e) / math.sqrt(HEAD_DIM)
    starts = [(w, w * SPAN, SPAN) for w in range(spans)] + [(spans, 0, TAIL)]

    @pl.loop(0, model // HEAD_DIM // UNROLL)
    def _(t):
        heads = [t * UNROLL + u for u in range(UNROLL)]
        cols = [pl.ds(pl.multiple_of(h * HEAD_DIM, HEAD_DIM), HEAD_DIM) for h in heads]
        vcols = [pl.ds(pl.multiple_of(model + h * HEAD_DIM, HEAD_DIM), HEAD_DIM) for h in heads]
        each = [(u, w, start, count) for u in range(UNROLL) for w, start, count in starts]
        s = [
            lax.dot_general(
                q_ref[start : start + count, cols[u]], kv_ref[w, :, cols[u]],
                (((1,), (1,)), ((), ())), preferred_element_type=jnp.float32,
            )
            for u, w, start, count in each
        ]
        top = [jnp.max(x, axis=-1, keepdims=True) for x in s]
        p = [jnp.exp2((x - m) * scale) for x, m in zip(s, top)]
        o = [
            jnp.dot(x.astype(jnp.bfloat16), kv_ref[w, :, vcols[u]], preferred_element_type=jnp.float32)
            for x, (u, w, _, _) in zip(p, each)
        ]
        o = [x / jnp.sum(y, axis=-1, keepdims=True) for x, y in zip(o, p)]
        first = lax.broadcasted_iota(jnp.int32, (TAIL, HEAD_DIM), 0) == 0
        for u in range(UNROLL):
            parts = o[u * windows : (u + 1) * windows]
            head = jnp.where(first, parts[-1], parts[0][:TAIL])
            full = jnp.concatenate([head, parts[0][TAIL:]] + parts[1:-1], 0)
            full = pltpu.roll(full, spans * SPAN - 1, 0)
            out_ref[:, cols[u]] = jnp.where(keep_ref[...] > 0.5, full, 0.0).astype(jnp.bfloat16)

    for copy in id_copies:
        copy.wait_send()
    for g in range(CHUNKS):
        total(g, (n - 2) * slots // 2, ring_send.at[g]).wait()
        total(g, n * slots // 2, pair_send.at[g]).wait()


def body(n, depth, queries, neighbours, w_key, w_value, retrieval_owner, retrieval_slot, doc_starts):
    span_count = doc_starts.shape[0]
    token_count, model = queries.shape
    slots, length, width = neighbours.shape
    windows = span_count + 1
    rows = length // CHUNKS
    chips = n // 2
    any_spec = pl.BlockSpec(memory_space=pl.ANY)
    vmem = pl.BlockSpec(memory_space=pltpu.VMEM)
    smem = pl.BlockSpec(memory_space=pltpu.SMEM)
    return pl.pallas_call(
        functools.partial(kernel, n, depth),
        out_shape=jax.ShapeDtypeStruct((token_count, model), jnp.bfloat16),
        in_specs=[smem, smem, smem, vmem, vmem] + [any_spec] * 4,
        out_specs=vmem,
        scratch_shapes=[pltpu.VMEM((n * slots, rows, width), jnp.bfloat16) for _ in range(CHUNKS)]
        + [
            pltpu.VMEM((width, 2 * model), jnp.bfloat16),
            pltpu.VMEM((windows, 2 * length, 2 * model), jnp.bfloat16),
            pltpu.VMEM((2 * windows, rows, width), jnp.bfloat16),
            pltpu.VMEM((token_count, model), jnp.bfloat16),
            pltpu.VMEM((token_count, model), jnp.bfloat16),
            pltpu.VMEM((token_count, HEAD_DIM), jnp.float32),
            pltpu.VMEM(retrieval_owner.shape, jnp.int32),
            pltpu.VMEM(retrieval_slot.shape, jnp.int32),
            pltpu.SMEM(retrieval_owner.shape, jnp.int32),
            pltpu.SMEM(retrieval_slot.shape, jnp.int32),
            pltpu.SemaphoreType.DMA((CHUNKS, chips // 2, 2)),
            pltpu.SemaphoreType.DMA((CHUNKS,)),
            pltpu.SemaphoreType.DMA((CHUNKS,)),
            pltpu.SemaphoreType.DMA((CHUNKS,)),
            pltpu.SemaphoreType.DMA((CHUNKS,)),
            pltpu.SemaphoreType.DMA((2,)),
            pltpu.SemaphoreType.DMA((2, 3)),
            pltpu.SemaphoreType.DMA,
        ],
        compiler_params=pltpu.CompilerParams(
            collective_id=0, has_side_effects=True, vmem_limit_bytes=60 * 1024 * 1024
        ),
    )(
        retrieval_owner, retrieval_slot, doc_starts, retrieval_owner, retrieval_slot,
        queries, neighbours, w_key, w_value,
    )


def solution(mesh):
    return jax.shard_map(
        functools.partial(body, mesh.shape["seq"], ring_depth(mesh)),
        mesh=mesh,
        in_specs=(
            P(("groups", "seq"), None),
            P(("groups", "seq"), None, None),
            P(),
            P(),
            P(("groups", "seq"), None),
            P(("groups", "seq"), None),
            P(("groups", "seq")),
        ),
        out_specs=P(("groups", "seq"), None),
        check_vma=False,
    )
```

```python
import functools
import math

import jax
import jax.numpy as jnp
from jax import lax
from jax.experimental import pallas as pl
from jax.experimental.pallas import tpu as pltpu
from jax.sharding import PartitionSpec as P

SPAN = 64
HEADS = 16
HEAD_DIM = 128
CHUNKS = 4
TAIL = 16
COLS = 1024
UNROLL = 4
STAGGER = 1


def ring_depth(mesh):
    devices = mesh.devices.reshape(mesh.shape["groups"], mesh.shape["seq"])[0]
    spots = [getattr(d, "coords", None) for d in devices[::2]]
    if any(s is None for s in spots) or len(spots) < 4:
        return 1
    spots = [tuple(s) for s in spots]
    apart = lambda a, b: {k for k in range(3) if a[k] != b[k]}
    return 2 if apart(spots[0], spots[1]).isdisjoint(apart(spots[0], spots[2])) else 1


def place_of(chip, chips, depth):
    if depth == 1:
        return chip
    far = chips // 2
    z, y = chip // 2, chip % 2
    return jnp.where(y == 0, z, 2 * far - 1 - z)


def chip_at(place, chips, depth):
    if depth == 1:
        return place
    far = chips // 2
    return jnp.where(place < far, 2 * place, 2 * (2 * far - 1 - place) + 1)


def kernel(
    n, depth,
    owner_s, slot_s, doc_s, owner_v, slot_v, q_hbm, nb_ref, wk_ref, wv_ref, out_ref,
    *scratch,
):
    gats = scratch[:CHUNKS]
    (w_ref, kv_ref, xn_ref, q_raw, q_ref, keep_ref, prev_ov, prev_sv, prev_os, prev_ss,
     ring_recv, ring_send, pair_recv, pair_send, own_sem, w_sem, id_sem, q_sem) = scratch[CHUNKS:]
    slots, length, width = nb_ref.shape
    rows = length // CHUNKS
    windows = kv_ref.shape[0]
    spans = windows - 1
    model = wk_ref.shape[1]
    chips = n // 2
    half = chips // 2

    me = lax.axis_index("seq")
    core = me % 2
    partner = me + 1 - 2 * core
    place = place_of(me // 2, chips, depth)

    def device_at(p):
        return chip_at((p + chips) % chips, chips, depth) * 2 + core

    right, left = device_at(place + 1), device_at(place - 1)
    nxt, prv = (me + 1) % n, (me + n - 1) % n

    w_copies = [
        pltpu.make_async_copy(wk_ref, w_ref.at[:, pl.ds(0, model)], w_sem.at[0]),
        pltpu.make_async_copy(wv_ref, w_ref.at[:, pl.ds(model, model)], w_sem.at[1]),
    ]
    own_copies = [
        pltpu.make_async_copy(
            nb_ref.at[:, pl.ds(g * rows, rows), :], gats[g].at[pl.ds(slots * me, slots)], own_sem.at[g]
        )
        for g in range(CHUNKS)
    ]

    q_copy = pltpu.make_async_copy(q_hbm, q_raw, q_sem)

    barrier = pltpu.get_barrier_semaphore()
    for other in (left, right, partner, nxt, prv):
        pl.semaphore_signal(barrier, inc=1, device_id={"seq": other}, device_id_type=pl.DeviceIdType.MESH)
    pl.semaphore_wait(barrier, 5)

    id_copies = [
        pltpu.make_async_remote_copy(
            src_ref=src, dst_ref=dst, send_sem=id_sem.at[k, 0], recv_sem=id_sem.at[k, 1],
            device_id={"seq": nxt}, device_id_type=pl.DeviceIdType.MESH,
        )
        for k, (src, dst) in enumerate(((owner_v, prev_ov), (slot_v, prev_sv)))
    ]
    id_moves = [
        pltpu.make_async_copy(prev_ov, prev_os, id_sem.at[0, 2]),
        pltpu.make_async_copy(prev_sv, prev_ss, id_sem.at[1, 2]),
    ]

    def share(g, origin, slot, count, own):
        block = origin * slots + slot
        if own:
            return nb_ref.at[pl.ds(slot, count), pl.ds(g * rows, rows), :], gats[g].at[pl.ds(block, count)]
        return gats[g].at[pl.ds(block, count)], gats[g].at[pl.ds(block, count)]

    def ring_copy(g, d, way):
        origin = device_at(place - (d - 1) if way == 0 else place + (d - 1))
        slot, count = (0, slots) if d < half else (way * slots // 2, slots // 2)
        src, dst = share(g, origin, slot, count, d == 1)
        return pltpu.make_async_remote_copy(
            src_ref=src, dst_ref=dst,
            send_sem=ring_send.at[g], recv_sem=ring_recv.at[g, d - 1, way],
            device_id={"seq": right if way == 0 else left}, device_id_type=pl.DeviceIdType.MESH,
        )

    def pair_copy(g, d, way):
        origin = device_at(place - d if way == 0 else place + d)
        slot, count = (0, slots) if d < half else (way * slots // 2, slots // 2)
        src, dst = share(g, origin, slot, count, d == 0)
        return pltpu.make_async_remote_copy(
            src_ref=src, dst_ref=dst,
            send_sem=pair_send.at[g], recv_sem=pair_recv.at[g],
            device_id={"seq": partner}, device_id_type=pl.DeviceIdType.MESH,
        )

    def event(g, d):
        if d == 0:
            for way in range(2):
                ring_copy(g, 1, way).start()
            pair_copy(g, 0, 0).start()
            own_copies[g].start()
            return
        for way in range(2):
            ring_copy(g, d, way).wait_recv()
            if d < half:
                ring_copy(g, d + 1, way).start()
            pair_copy(g, d, way).start()

    def total(g, blocks, sem):
        part = gats[g].at[pl.ds(0, blocks)]
        return pltpu.make_async_copy(part, part, sem)

    def norm_piece(g):
        own_copies[g].wait()
        total(g, n * slots // 2, pair_recv.at[g]).wait()

        @pl.loop(0, 2 * windows)
        def _(i):
            span, j = jnp.maximum(i // 2 - 1, 0), i % 2
            before = prev_os[j, spans - 1] * slots + prev_ss[j, spans - 1]
            mine = owner_s[j, span] * slots + slot_s[j, span]
            x = gats[g][jnp.where(i < 2, before, mine)].astype(jnp.float32)
            factor = lax.rsqrt(jnp.mean(x * x, axis=-1, keepdims=True) + 1e-06)
            xn_ref[i] = (x * factor).astype(jnp.bfloat16)

    def proj_piece(g, part):
        xs = xn_ref.reshape(windows * 2 * rows, width)

        @pl.loop(0, model // COLS)
        def _(c):
            cols = pl.ds(pl.multiple_of(part * model + c * COLS, COLS), COLS)
            y = jnp.dot(xs[...], w_ref[:, cols], preferred_element_type=jnp.float32).astype(jnp.bfloat16)
            kv_ref[:, g * 2 * rows : (g + 1) * 2 * rows, cols] = y.reshape(windows, 2 * rows, COLS)

    def shift_piece():
        q_copy.wait()

        @pl.loop(0, model // COLS)
        def _(c):
            cols = pl.ds(pl.multiple_of(c * COLS, COLS), COLS)
            q_ref[:, cols] = pltpu.roll(q_raw[:, cols].astype(jnp.float32), 1, 0).astype(jnp.bfloat16)

        at = lax.broadcasted_iota(jnp.int32, (SPAN, HEAD_DIM), 0)
        for c in range(spans):
            open_row = (1 - doc_s[c]).astype(jnp.float32)
            if c == 0:
                open_row = jnp.where(me == 0, 0.0, open_row)
            keep_ref[c * SPAN : (c + 1) * SPAN, :] = jnp.where(at == SPAN - 1, 1.0, open_row)

    def id_piece():
        for copy, move in zip(id_copies, id_moves):
            copy.wait_recv()
            move.start()
        for move in id_moves:
            move.wait()
        for c in w_copies:
            c.wait()

    order = sorted(
        ((STAGGER * g + d, g, d) for g in range(CHUNKS) for d in range(half + 1)),
    )
    for copy in id_copies:
        copy.start()
    pending = []
    for at, (_, g, d) in enumerate(order):
        event(g, d)
        if at == 0:
            q_copy.start()
            for c in w_copies:
                c.start()
            pending = [shift_piece, id_piece]
        elif pending:
            pending.pop(0)()
        if d == half:
            pending += [
                functools.partial(norm_piece, g),
                functools.partial(proj_piece, g, 0),
                functools.partial(proj_piece, g, 1),
            ]
    for piece in pending:
        piece()

    scale = math.log2(math.e) / math.sqrt(HEAD_DIM)
    starts = [(w, w * SPAN, SPAN) for w in range(spans)] + [(spans, 0, TAIL)]

    @pl.loop(0, model // HEAD_DIM // UNROLL)
    def _(t):
        heads = [t * UNROLL + u for u in range(UNROLL)]
        cols = [pl.ds(pl.multiple_of(h * HEAD_DIM, HEAD_DIM), HEAD_DIM) for h in heads]
        vcols = [pl.ds(pl.multiple_of(model + h * HEAD_DIM, HEAD_DIM), HEAD_DIM) for h in heads]
        each = [(u, w, start, count) for u in range(UNROLL) for w, start, count in starts]
        s = [
            lax.dot_general(
                q_ref[start : start + count, cols[u]], kv_ref[w, :, cols[u]],
                (((1,), (1,)), ((), ())), preferred_element_type=jnp.float32,
            )
            for u, w, start, count in each
        ]
        top = [jnp.max(x, axis=-1, keepdims=True) for x in s]
        p = [jnp.exp2((x - m) * scale) for x, m in zip(s, top)]
        o = [
            jnp.dot(x.astype(jnp.bfloat16), kv_ref[w, :, vcols[u]], preferred_element_type=jnp.float32)
            for x, (u, w, _, _) in zip(p, each)
        ]
        o = [x / jnp.sum(y, axis=-1, keepdims=True) for x, y in zip(o, p)]
        first = lax.broadcasted_iota(jnp.int32, (TAIL, HEAD_DIM), 0) == 0
        for u in range(UNROLL):
            parts = o[u * windows : (u + 1) * windows]
            head = jnp.where(first, parts[-1], parts[0][:TAIL])
            full = jnp.concatenate([head, parts[0][TAIL:]] + parts[1:-1], 0)
            full = pltpu.roll(full, spans * SPAN - 1, 0)
            out_ref[:, cols[u]] = jnp.where(keep_ref[...] > 0.5, full, 0.0).astype(jnp.bfloat16)

    for copy in id_copies:
        copy.wait_send()
    for g in range(CHUNKS):
        total(g, (n - 2) * slots // 2, ring_send.at[g]).wait()
        total(g, n * slots // 2, pair_send.at[g]).wait()


def body(n, depth, queries, neighbours, w_key, w_value, retrieval_owner, retrieval_slot, doc_starts):
    span_count = doc_starts.shape[0]
    token_count, model = queries.shape
    slots, length, width = neighbours.shape
    windows = span_count + 1
    rows = length // CHUNKS
    chips = n // 2
    owner_rows, slot_rows = retrieval_owner.T, retrieval_slot.T
    any_spec = pl.BlockSpec(memory_space=pl.ANY)
    vmem = pl.BlockSpec(memory_space=pltpu.VMEM)
    smem = pl.BlockSpec(memory_space=pltpu.SMEM)
    return pl.pallas_call(
        functools.partial(kernel, n, depth),
        out_shape=jax.ShapeDtypeStruct((token_count, model), jnp.bfloat16),
        in_specs=[smem, smem, smem, vmem, vmem] + [any_spec] * 4,
        out_specs=vmem,
        scratch_shapes=[pltpu.VMEM((n * slots, rows, width), jnp.bfloat16) for _ in range(CHUNKS)]
        + [
            pltpu.VMEM((width, 2 * model), jnp.bfloat16),
            pltpu.VMEM((windows, 2 * length, 2 * model), jnp.bfloat16),
            pltpu.VMEM((2 * windows, rows, width), jnp.bfloat16),
            pltpu.VMEM((token_count, model), jnp.bfloat16),
            pltpu.VMEM((token_count, model), jnp.bfloat16),
            pltpu.VMEM((token_count, HEAD_DIM), jnp.float32),
            pltpu.VMEM(owner_rows.shape, jnp.int32),
            pltpu.VMEM(slot_rows.shape, jnp.int32),
            pltpu.SMEM(owner_rows.shape, jnp.int32),
            pltpu.SMEM(slot_rows.shape, jnp.int32),
            pltpu.SemaphoreType.DMA((CHUNKS, chips // 2, 2)),
            pltpu.SemaphoreType.DMA((CHUNKS,)),
            pltpu.SemaphoreType.DMA((CHUNKS,)),
            pltpu.SemaphoreType.DMA((CHUNKS,)),
            pltpu.SemaphoreType.DMA((CHUNKS,)),
            pltpu.SemaphoreType.DMA((2,)),
            pltpu.SemaphoreType.DMA((2, 3)),
            pltpu.SemaphoreType.DMA,
        ],
        compiler_params=pltpu.CompilerParams(
            collective_id=0, has_side_effects=True, vmem_limit_bytes=60 * 1024 * 1024
        ),
    )(
        owner_rows, slot_rows, doc_starts, owner_rows, slot_rows,
        queries, neighbours, w_key, w_value,
    )


def solution(mesh):
    return jax.shard_map(
        functools.partial(body, mesh.shape["seq"], ring_depth(mesh)),
        mesh=mesh,
        in_specs=(
            P(("groups", "seq"), None),
            P(("groups", "seq"), None, None),
            P(),
            P(),
            P(("groups", "seq"), None),
            P(("groups", "seq"), None),
            P(("groups", "seq")),
        ),
        out_specs=P(("groups", "seq"), None),
        check_vma=False,
    )
```
